32 devices in a mesh: strip: 8 (over z, x), wave: 4 (over y, core).
Axes of the slice: x: 2, y: 2, z: 4, core: 2. Of those that a mesh axis runs over, the one named last changes fastest.
Arguments:
- source: bfloat16 [16, 1024, 2, 512], P('strip', None, None, 'wave'), parts along dimension 3, may hold values from -4 to 4
- pivot_inverse_real: bfloat16 [16, 4096, 1024], P('strip', 'wave'), parts along dimension 1, may hold values from -1 to 1
- factor_imag: bfloat16 [16, 4096, 1024], P('strip', 'wave'), parts along dimension 1, may hold values from -1 to 1
Outputs:
- solution: bfloat16 [16, 1024, 2, 512], P('strip', None, None, 'wave'), parts along dimension 3
The draws below stay inside these ranges and needn't reach their ends.
There are 4 independent parts, one for each index of `wave`. The reference program is written for one: setup_inputs(seed, part) draws one part's arguments, and reference() takes and returns one part's arrays. A program takes and returns all parts, laid end to end along the dimension named above; each array names one. Nothing has to cross between parts.
All inputs are finite; a program needn't handle non-finite values.
Results may differ from the reference program's by a relative error of at most 0.033.
Values may be sent and summed in bfloat16 or wider, within the bound.
A program may use at most 64 MiB of HBM per device.

```python
import jax
import jax.numpy as jnp
from jax import lax

NY = 1024
RHS = 128
LAYER_TOTAL = 16


def factor_parts(key):
    draw_keys = jax.random.split(jax.random.fold_in(key, 31), 8)
    slow_share = 0.5
    slow_mode = jax.random.bernoulli(draw_keys[0], slow_share, (NY,))
    spread = jnp.exp(jax.random.uniform(draw_keys[1], (LAYER_TOTAL, NY), jnp.float32, -0.7, 0.7))
    fast_rate = jnp.exp(jax.random.uniform(draw_keys[2], (NY,), jnp.float32, jnp.log(1.0 / 20.0), jnp.log(1.0 / 8.0)))
    attenuation_factor = jnp.where(slow_mode, 1.0 / LAYER_TOTAL, fast_rate)[None, :] * spread
    surge_events = jax.random.bernoulli(draw_keys[3], 3.0 / LAYER_TOTAL, (LAYER_TOTAL, 1))
    surge_damping = jax.random.uniform(draw_keys[4], (LAYER_TOTAL, 1), jnp.float32, 0.5, 0.8)
    amplitude_level = 0.98 * jnp.exp(-attenuation_factor) * jnp.where(surge_events, surge_damping, 1.0)
    phases = jax.random.uniform(draw_keys[5], (LAYER_TOTAL, NY), jnp.float32, -jnp.pi, jnp.pi)
    mixing = 0.2 / jnp.sqrt(2.0 * NY)
    identity = jnp.eye(NY, dtype=jnp.float32)
    off_diagonal = 1.0 - identity
    real_noise = jnp.clip(jax.random.normal(draw_keys[6], (LAYER_TOTAL, NY, NY), jnp.float32), -6.0, 6.0)
    imag_noise = jnp.clip(jax.random.normal(draw_keys[7], (LAYER_TOTAL, NY, NY), jnp.float32), -6.0, 6.0)
    real_part = real_noise * mixing * off_diagonal + identity[None] * (amplitude_level * jnp.cos(phases))[:, None, :]
    imag_part = imag_noise * mixing * off_diagonal + identity[None] * (amplitude_level * jnp.sin(phases))[:, None, :]
    return (real_part, imag_part)


def draw_pivot_inverse_real(key, part):
    real_part, imag_part = factor_parts(key)
    return real_part.astype(jnp.bfloat16)


def draw_factor_imag(key, part):
    real_part, imag_part = factor_parts(key)
    return imag_part.astype(jnp.bfloat16)


def steps_of(stream_key, dims, cuts, low, largest):
    def one(dim, parts):
        heights = jax.random.uniform(jax.random.fold_in(jax.random.fold_in(stream_key, 6), dim), (parts,), jnp.float32, low / len(cuts), largest / len(cuts))
        return jnp.repeat(jnp.exp(heights), dims[dim] // parts).reshape((-1,) + (1,) * (len(dims) - dim - 1))

    factor_of = one(*cuts[0])
    for cut in cuts[1:]:
        factor_of = factor_of * one(*cut)
    return factor_of


def scatter_about(rng, extent, deviation, reach, cuts=(), held_as=jnp.bfloat16):
    loudness = steps_of(rng, extent, cuts, -0.22, 0.18) if cuts else 1.0
    array = jax.random.normal(rng, extent, jnp.float32) * deviation * loudness
    return jnp.minimum(jnp.maximum(array, -reach), reach).astype(held_as)


def setup_inputs(seed: int = 0, part: int = 0) -> dict:
    streams_of = jax.random.split(jax.random.key(seed), 4)
    part_keys = jax.random.split(jax.random.fold_in(streams_of[3], part), 4)
    source = scatter_about(part_keys[0], (LAYER_TOTAL, NY, 2, RHS), 0.25, 4.0, ((0, 8),))
    pivot_inverse_real = draw_pivot_inverse_real(jax.random.fold_in(jax.random.fold_in(streams_of[3], part), 71), part)
    factor_imag = draw_factor_imag(jax.random.fold_in(jax.random.fold_in(streams_of[3], part), 71), part)
    return {"source": source, "pivot_inverse_real": pivot_inverse_real, "factor_imag": factor_imag}


def complex_apply(real_part, imag_part, vector):
    mode_count, halves, columns = vector.shape
    merged = vector.reshape(mode_count, halves * columns)
    direct = jnp.dot(real_part, merged, preferred_element_type=jnp.float32).reshape(mode_count, halves, columns)
    crossed = jnp.dot(imag_part, merged, preferred_element_type=jnp.float32).reshape(mode_count, halves, columns)
    return jnp.stack([direct[:, 0] - crossed[:, 1], direct[:, 1] + crossed[:, 0]], axis=1)


def reference(source, pivot_inverse_real, factor_imag):
    def forward(trace_before, inputs):
        layer_source, real_part, imag_part = inputs
        summed = (layer_source.astype(jnp.float32) + trace_before).astype(jnp.bfloat16)
        trace_after = complex_apply(real_part, imag_part, summed)
        return trace_after, trace_after

    initial = jnp.zeros(source.shape[1:], jnp.float32)
    unused, traces = lax.scan(forward, initial, (source, pivot_inverse_real, factor_imag))

    def backward(updated_field, inputs):
        trace_here, real_part, imag_part = inputs
        field_now = trace_here + complex_apply(real_part, imag_part, updated_field.astype(jnp.bfloat16))
        return field_now, field_now

    unused, fields = lax.scan(backward, initial, (traces, pivot_inverse_real, factor_imag), reverse=True)
    return fields.astype(jnp.bfloat16)
```

```python
import functools

import jax
import jax.numpy as jnp
from jax import lax
from jax.experimental import pallas as pl
from jax.experimental.pallas import tpu as pltpu
from jax.sharding import PartitionSpec as P

BATCHES = 8
BLOCK = 256
F32 = jnp.float32
BF16 = jnp.bfloat16
MESH = pl.DeviceIdType.MESH
PLAIN = (((1,), (0,)), ((), ()))
ACROSS = (((1,), (1,)), ((), ()))


def complex_rows(vectors, real_part, imag_part, dims):
    chunks, rows, modes = vectors.shape
    merged = vectors.reshape(chunks * rows, modes)
    split = (chunks, 2, rows // 2, modes)
    direct = lax.dot_general(merged, real_part, dims, preferred_element_type=F32).reshape(split)
    crossed = lax.dot_general(merged, imag_part, dims, preferred_element_type=F32).reshape(split)
    both = jnp.concatenate([direct[:, :1] - crossed[:, 1:], direct[:, 1:] + crossed[:, :1]], axis=1)
    return both.reshape(chunks, rows, modes)


def kernel(
    strips, src_hbm, pr_hbm, pi_hbm, out, src, pr, pi, fwd_r, fwd_i, bwd_r, bwd_i, last_trace, base,
    fin, fout, bin_, bout, load_sem, fsend, frecv, bsend, brecv,
):
    me = lax.axis_index("strip")
    batches, rows, modes = fin.shape
    is_first, is_last = me == 0, me == strips - 1
    after, before = jnp.minimum(me + 1, strips - 1), jnp.maximum(me - 1, 0)
    barrier = pltpu.get_barrier_semaphore()

    @pl.when(jnp.logical_not(is_first))
    def _():
        pl.semaphore_signal(barrier, inc=1, device_id={"strip": before}, device_id_type=MESH)

    @pl.when(jnp.logical_not(is_last))
    def _():
        pl.semaphore_signal(barrier, inc=1, device_id={"strip": after}, device_id_type=MESH)

    loads = [
        pltpu.make_async_copy(source.at[layer], target.at[layer], load_sem.at[3 * layer + which])
        for layer in range(2)
        for which, (source, target) in enumerate(((src_hbm, src), (pr_hbm, pr), (pi_hbm, pi)))
    ]
    for load in loads:
        load.start()

    def forward_copy(b):
        return pltpu.make_async_remote_copy(
            src_ref=fout.at[b], dst_ref=fin.at[b], send_sem=fsend.at[b], recv_sem=frecv.at[b],
            device_id={"strip": after}, device_id_type=MESH,
        )

    def backward_copy(b):
        return pltpu.make_async_remote_copy(
            src_ref=bout.at[b], dst_ref=bin_.at[b], send_sem=bsend.at[b], recv_sem=brecv.at[b],
            device_id={"strip": before}, device_id_type=MESH,
        )

    for load in loads[:3]:
        load.wait()
    trace = complex_rows(src[0], pr[0], pi[0], ACROSS)
    for load in loads[3:]:
        load.wait()
    summed = (src[1].astype(F32) + trace).astype(BF16)
    last_trace[...] = complex_rows(summed, pr[1], pi[1], ACROSS)

    inner = jnp.logical_not(jnp.logical_or(is_first, is_last))

    @pl.when(inner)
    def _():
        pl.semaphore_wait(barrier, 2)

    @pl.when(jnp.logical_not(inner))
    def _():
        pl.semaphore_wait(barrier, 1)

    def each(body):
        def step(b, carry):
            body(b)
            return carry

        lax.fori_loop(0, batches, step, 0)

    @pl.when(is_first)
    def _():
        @each
        def _(b):
            fout[b] = last_trace[b].astype(BF16)
            forward_copy(b).start()

    def product_rows(left_r, left_i, right_r, right_i):
        real = jnp.dot(left_r, right_r, preferred_element_type=F32) - jnp.dot(
            left_i, right_i, preferred_element_type=F32
        )
        imag = jnp.dot(left_r, right_i, preferred_element_type=F32) + jnp.dot(
            left_i, right_r, preferred_element_type=F32
        )
        return real, imag

    def build(target_r, target_i, compute):
        def step(i, carry):
            block = pl.ds(pl.multiple_of(i * BLOCK, BLOCK), BLOCK)
            real, imag = compute(block)
            target_r[:, block] = real.T.astype(BF16)
            target_i[:, block] = imag.T.astype(BF16)
            return carry

        lax.fori_loop(0, modes // BLOCK, step, 0)

    def forward_rows(block):
        return product_rows(pr[1, block, :], pi[1, block, :], pr[0], pi[0])

    def backward_rows(block):
        return product_rows(pr[0, block, :], pi[0, block, :], pr[1], pi[1])

    def turn_rows(block):
        real, imag = backward_rows(block)
        real, imag = product_rows(real.astype(BF16), imag.astype(BF16), pr[0], pi[0])
        return real + pr[0, block, :].astype(F32), imag + pi[0, block, :].astype(F32)

    early = me < strips // 2

    @pl.when(inner)
    def _():
        build(fwd_r, fwd_i, forward_rows)

    @pl.when(jnp.logical_and(inner, jnp.logical_not(early)))
    def _():
        build(bwd_r, bwd_i, backward_rows)

    @pl.when(inner)
    def _():
        @each
        def _(b):
            forward_copy(b).wait_recv()
            total = last_trace[b] + complex_rows(fin[b][None], fwd_r[...], fwd_i[...], PLAIN)[0]
            fout[b] = total.astype(BF16)
            forward_copy(b).start()
            last_trace[b] = total

    @pl.when(is_last)
    def _():
        build(bwd_r, bwd_i, turn_rows)
        known = src[0].astype(F32) + last_trace[...]
        base[...] = complex_rows(known.astype(BF16), pr[0], pi[0], ACROSS)

        @each
        def _(b):
            forward_copy(b).wait_recv()
            total = base[b] + complex_rows(fin[b][None], bwd_r[...], bwd_i[...], PLAIN)[0]
            bout[b] = total.astype(BF16)
            backward_copy(b).start()
            out[0, b] = total.astype(BF16)

        passed = complex_rows(fin[...], pr[0], pi[0], ACROSS).astype(BF16)
        field = last_trace[...] + complex_rows(passed, pr[1], pi[1], ACROSS)
        out[1] = field.astype(BF16)

    @pl.when(inner)
    def _():
        known = src[0].astype(F32) + fin[...].astype(F32) + last_trace[...]
        base[...] = complex_rows(known.astype(BF16), pr[0], pi[0], ACROSS)

    @pl.when(is_first)
    def _():
        known = src[0].astype(F32) + last_trace[...]
        base[...] = complex_rows(known.astype(BF16), pr[0], pi[0], ACROSS)

    @pl.when(jnp.logical_and(early, jnp.logical_not(is_last)))
    def _():
        build(bwd_r, bwd_i, backward_rows)

    @pl.when(jnp.logical_not(is_last))
    def _():
        @each
        def _(b):
            backward_copy(b).wait_recv()
            total = base[b] + complex_rows(bin_[b][None], bwd_r[...], bwd_i[...], PLAIN)[0]
            field = total.astype(BF16)
            out[0, b] = field

            @pl.when(jnp.logical_not(is_first))
            def _():
                bout[b] = field
                backward_copy(b).start()

        field = last_trace[...] + complex_rows(bin_[...], pr[1], pi[1], ACROSS)
        out[1] = field.astype(BF16)

        @each
        def _(b):
            forward_copy(b).wait_send()

    @pl.when(jnp.logical_not(is_first))
    def _():
        @each
        def _(b):
            backward_copy(b).wait_send()


def solution(mesh):
    strips = mesh.shape["strip"]

    def step(source, pivot_inverse_real, factor_imag):
        layers, modes, halves, columns = source.shape
        width = columns // BATCHES
        rows = halves * width
        chunked = (layers, BATCHES, rows, modes)
        placed = source.reshape(layers, modes, halves, BATCHES, width)
        placed = placed.transpose(0, 3, 2, 4, 1).reshape(chunked)
        anywhere = pl.BlockSpec(memory_space=pl.ANY)
        vectors = (BATCHES, rows, modes)
        square = (modes, modes)
        result = pl.pallas_call(
            functools.partial(kernel, strips),
            out_shape=jax.ShapeDtypeStruct(chunked, BF16),
            in_specs=[anywhere] * 3,
            out_specs=pl.BlockSpec(memory_space=pltpu.VMEM),
            scratch_shapes=[
                pltpu.VMEM(chunked, BF16),
                pltpu.VMEM((layers,) + square, BF16),
                pltpu.VMEM((layers,) + square, BF16),
            ]
            + [pltpu.VMEM(square, BF16)] * 4
            + [pltpu.VMEM(vectors, F32)] * 2
            + [pltpu.VMEM(vectors, BF16)] * 4
            + [pltpu.SemaphoreType.DMA((6,))]
            + [pltpu.SemaphoreType.DMA((BATCHES,))] * 4,
            compiler_params=pltpu.CompilerParams(
                collective_id=0, has_side_effects=True, vmem_limit_bytes=56 * 1024 * 1024
            ),
        )(placed, pivot_inverse_real, factor_imag)
        result = result.reshape(layers, BATCHES, halves, width, modes)
        return result.transpose(0, 4, 2, 1, 3).reshape(source.shape)

    return jax.shard_map(
        step,
        mesh=mesh,
        in_specs=(P("strip", None, None, "wave"), P("strip", "wave", None), P("strip", "wave", None)),
        out_specs=P("strip", None, None, "wave"),
        check_vma=False,
    )
```

```python
import functools

import jax
import jax.numpy as jnp
from jax import lax
from jax.experimental import pallas as pl
from jax.experimental.pallas import tpu as pltpu
from jax.sharding import PartitionSpec as P

BATCHES = 8
PIECES = 2
BLOCK = 256
F32 = jnp.float32
BF16 = jnp.bfloat16
MESH = pl.DeviceIdType.MESH
PLAIN = (((1,), (0,)), ((), ()))
ACROSS = (((1,), (1,)), ((), ()))


def combine(direct, crossed):
    return jnp.stack([direct[0] - crossed[1], direct[1] + crossed[0]])


def complex_rows(vectors, real_part, imag_part, dims):
    halves, columns, modes = vectors.shape
    merged = vectors.reshape(halves * columns, modes)
    outcome = (halves, columns, real_part.shape[1 - dims[0][1][0]])
    direct = lax.dot_general(merged, real_part, dims, preferred_element_type=F32).reshape(outcome)
    crossed = lax.dot_general(merged, imag_part, dims, preferred_element_type=F32).reshape(outcome)
    return combine(direct, crossed)


def kernel(
    strips, src_hbm, pr_hbm, pi_hbm, out, src, pr, pi, fwd_r, fwd_i, bwd_r, bwd_i, last_trace, base,
    fin, fout, bin_, bout, load_sem, fsend, frecv, bsend, brecv,
):
    me = lax.axis_index("strip")
    halves, columns, modes = fin.shape
    batches = BATCHES
    width = columns // batches
    depth = modes // PIECES
    is_first, is_last = me == 0, me == strips - 1
    after, before = jnp.minimum(me + 1, strips - 1), jnp.maximum(me - 1, 0)
    barrier = pltpu.get_barrier_semaphore()

    @pl.when(jnp.logical_not(is_first))
    def _():
        pl.semaphore_signal(barrier, inc=1, device_id={"strip": before}, device_id_type=MESH)

    @pl.when(jnp.logical_not(is_last))
    def _():
        pl.semaphore_signal(barrier, inc=1, device_id={"strip": after}, device_id_type=MESH)

    loads = [
        pltpu.make_async_copy(source.at[layer], target.at[layer], load_sem.at[3 * layer + which])
        for layer in range(2)
        for which, (source, target) in enumerate(((src_hbm, src), (pr_hbm, pr), (pi_hbm, pi)))
    ]
    for load in loads:
        load.start()

    def columns_of(b):
        return pl.ds(pl.multiple_of(b * width, width), width)

    def modes_of(piece):
        return pl.ds(piece * depth, depth)

    def forward_copy(b, piece):
        part = (slice(None), columns_of(b), modes_of(piece))
        return pltpu.make_async_remote_copy(
            src_ref=fout.at[part], dst_ref=fin.at[part],
            send_sem=fsend.at[b * PIECES + piece], recv_sem=frecv.at[b * PIECES + piece],
            device_id={"strip": after}, device_id_type=MESH,
        )

    def backward_copy(b, piece):
        part = (slice(None), columns_of(b), modes_of(piece))
        return pltpu.make_async_remote_copy(
            src_ref=bout.at[part], dst_ref=bin_.at[part],
            send_sem=bsend.at[b * PIECES + piece], recv_sem=brecv.at[b * PIECES + piece],
            device_id={"strip": before}, device_id_type=MESH,
        )

    def pass_on(b, copy, arriving, known, real_part, imag_part, emit):
        part = columns_of(b)
        total = known[:, part, :]
        for piece in range(PIECES - 1):
            copy(b, piece).wait_recv()
            total = total + complex_rows(
                arriving[:, part, modes_of(piece)],
                real_part[modes_of(piece), :], imag_part[modes_of(piece), :], PLAIN,
            )
        copy(b, PIECES - 1).wait_recv()
        ending = modes_of(PIECES - 1)
        vectors = arriving[:, part, ending]
        for piece in range(PIECES):
            lanes = modes_of(piece)
            emit(
                piece, (slice(None), part, lanes),
                total[:, :, piece * depth : (piece + 1) * depth]
                + complex_rows(vectors, real_part[ending, lanes], imag_part[ending, lanes], PLAIN),
            )

    for load in loads[:3]:
        load.wait()
    trace = complex_rows(src[0], pr[0], pi[0], ACROSS)
    for load in loads[3:]:
        load.wait()
    summed = (src[1].astype(F32) + trace).astype(BF16)
    last_trace[...] = complex_rows(summed, pr[1], pi[1], ACROSS)

    inner = jnp.logical_not(jnp.logical_or(is_first, is_last))

    @pl.when(inner)
    def _():
        pl.semaphore_wait(barrier, 2)

    @pl.when(jnp.logical_not(inner))
    def _():
        pl.semaphore_wait(barrier, 1)

    def each(body):
        def step(b, carry):
            body(b)
            return carry

        lax.fori_loop(0, batches, step, 0)

    @pl.when(is_first)
    def _():
        @each
        def _(b):
            part = columns_of(b)
            fout[:, part, :] = last_trace[:, part, :].astype(BF16)
            for piece in range(PIECES):
                forward_copy(b, piece).start()

    def product_rows(left_r, left_i, right_r, right_i):
        real = jnp.dot(left_r, right_r, preferred_element_type=F32) - jnp.dot(
            left_i, right_i, preferred_element_type=F32
        )
        imag = jnp.dot(left_r, right_i, preferred_element_type=F32) + jnp.dot(
            left_i, right_r, preferred_element_type=F32
        )
        return real, imag

    def build(target_r, target_i, compute):
        def step(i, carry):
            block = pl.ds(pl.multiple_of(i * BLOCK, BLOCK), BLOCK)
            real, imag = compute(block)
            target_r[:, block] = real.T.astype(BF16)
            target_i[:, block] = imag.T.astype(BF16)
            return carry

        lax.fori_loop(0, modes // BLOCK, step, 0)

    def forward_rows(block):
        return product_rows(pr[1, block, :], pi[1, block, :], pr[0], pi[0])

    def backward_rows(block):
        return product_rows(pr[0, block, :], pi[0, block, :], pr[1], pi[1])

    def turn_rows(block):
        real, imag = backward_rows(block)
        real, imag = product_rows(real.astype(BF16), imag.astype(BF16), pr[0], pi[0])
        return real + pr[0, block, :].astype(F32), imag + pi[0, block, :].astype(F32)

    early = me < strips // 2

    @pl.when(inner)
    def _():
        build(fwd_r, fwd_i, forward_rows)

    @pl.when(jnp.logical_and(inner, jnp.logical_not(early)))
    def _():
        build(bwd_r, bwd_i, backward_rows)

    @pl.when(inner)
    def _():
        @each
        def _(b):
            def emit(piece, part, total):
                fout[part] = total.astype(BF16)
                forward_copy(b, piece).start()
                last_trace[part] = total

            pass_on(b, forward_copy, fin, last_trace, fwd_r, fwd_i, emit)

    @pl.when(is_last)
    def _():
        build(bwd_r, bwd_i, turn_rows)
        known = src[0].astype(F32) + last_trace[...]
        base[...] = complex_rows(known.astype(BF16), pr[0], pi[0], ACROSS)

        @each
        def _(b):
            def emit(piece, part, total):
                field = total.astype(BF16)
                bout[part] = field
                backward_copy(b, piece).start()
                out[(0,) + part] = field

            pass_on(b, forward_copy, fin, base, bwd_r, bwd_i, emit)

        passed = complex_rows(fin[...], pr[0], pi[0], ACROSS).astype(BF16)
        field = last_trace[...] + complex_rows(passed, pr[1], pi[1], ACROSS)
        out[1] = field.astype(BF16)

    @pl.when(inner)
    def _():
        known = src[0].astype(F32) + fin[...].astype(F32) + last_trace[...]
        base[...] = complex_rows(known.astype(BF16), pr[0], pi[0], ACROSS)

    @pl.when(is_first)
    def _():
        known = src[0].astype(F32) + last_trace[...]
        base[...] = complex_rows(known.astype(BF16), pr[0], pi[0], ACROSS)

    @pl.when(jnp.logical_and(early, jnp.logical_not(is_last)))
    def _():
        build(bwd_r, bwd_i, backward_rows)

    @pl.when(jnp.logical_not(is_last))
    def _():
        @each
        def _(b):
            def emit(piece, part, total):
                field = total.astype(BF16)

                @pl.when(jnp.logical_not(is_first))
                def _():
                    bout[part] = field
                    backward_copy(b, piece).start()

                out[(0,) + part] = field

            pass_on(b, backward_copy, bin_, base, bwd_r, bwd_i, emit)

        field = last_trace[...] + complex_rows(bin_[...], pr[1], pi[1], ACROSS)
        out[1] = field.astype(BF16)

        @each
        def _(b):
            for piece in range(PIECES):
                forward_copy(b, piece).wait_send()

    @pl.when(jnp.logical_not(is_first))
    def _():
        @each
        def _(b):
            for piece in range(PIECES):
                backward_copy(b, piece).wait_send()


def solution(mesh):
    strips = mesh.shape["strip"]

    def step(source, pivot_inverse_real, factor_imag):
        layers, modes, halves, columns = source.shape
        placed = source.transpose(0, 2, 3, 1)
        anywhere = pl.BlockSpec(memory_space=pl.ANY)
        vectors = (halves, columns, modes)
        chunked = (layers,) + vectors
        square = (modes, modes)
        result = pl.pallas_call(
            functools.partial(kernel, strips),
            out_shape=jax.ShapeDtypeStruct(chunked, BF16),
            in_specs=[anywhere] * 3,
            out_specs=pl.BlockSpec(memory_space=pltpu.VMEM),
            scratch_shapes=[
                pltpu.VMEM(chunked, BF16),
                pltpu.VMEM((layers,) + square, BF16),
                pltpu.VMEM((layers,) + square, BF16),
            ]
            + [pltpu.VMEM(square, BF16)] * 4
            + [pltpu.VMEM(vectors, F32)] * 2
            + [pltpu.VMEM(vectors, BF16)] * 4
            + [pltpu.SemaphoreType.DMA((6,))]
            + [pltpu.SemaphoreType.DMA((BATCHES * PIECES,))] * 4,
            compiler_params=pltpu.CompilerParams(
                collective_id=0, has_side_effects=True, vmem_limit_bytes=56 * 1024 * 1024
            ),
        )(placed, pivot_inverse_real, factor_imag)
        return result.transpose(0, 3, 1, 2)

    return jax.shard_map(
        step,
        mesh=mesh,
        in_specs=(P("strip", None, None, "wave"), P("strip", "wave", None), P("strip", "wave", None)),
        out_specs=P("strip", None, None, "wave"),
        check_vma=False,
    )
```

```python
import functools

import jax
import jax.numpy as jnp
from jax import lax
from jax.experimental import pallas as pl
from jax.experimental.pallas import tpu as pltpu
from jax.sharding import PartitionSpec as P

BATCHES = 8
PIECES = 2
GROUP = 2
BLOCK = 256
F32 = jnp.float32
BF16 = jnp.bfloat16
MESH = pl.DeviceIdType.MESH
PLAIN = (((1,), (0,)), ((), ()))
ACROSS = (((1,), (1,)), ((), ()))


def combine(direct, crossed):
    return jnp.stack([direct[0] - crossed[1], direct[1] + crossed[0]])


def complex_rows(vectors, real_part, imag_part, dims):
    halves, columns, modes = vectors.shape
    merged = vectors.reshape(halves * columns, modes)
    outcome = (halves, columns, real_part.shape[1 - dims[0][1][0]])
    direct = lax.dot_general(merged, real_part, dims, preferred_element_type=F32).reshape(outcome)
    crossed = lax.dot_general(merged, imag_part, dims, preferred_element_type=F32).reshape(outcome)
    return combine(direct, crossed)


def kernel(
    strips, src_hbm, pr_hbm, pi_hbm, out, src, pr, pi, fwd_r, fwd_i, bwd_r, bwd_i, last_trace, base,
    fin, fout, bin_, bout, load_sem, fsend, frecv, bsend, brecv,
):
    me = lax.axis_index("strip")
    halves, columns, modes = fin.shape
    batches = BATCHES
    width = columns // batches
    depth = modes // PIECES
    is_first, is_last = me == 0, me == strips - 1
    after, before = jnp.minimum(me + 1, strips - 1), jnp.maximum(me - 1, 0)
    barrier = pltpu.get_barrier_semaphore()

    @pl.when(jnp.logical_not(is_first))
    def _():
        pl.semaphore_signal(barrier, inc=1, device_id={"strip": before}, device_id_type=MESH)

    @pl.when(jnp.logical_not(is_last))
    def _():
        pl.semaphore_signal(barrier, inc=1, device_id={"strip": after}, device_id_type=MESH)

    loads = [
        pltpu.make_async_copy(source.at[layer], target.at[layer], load_sem.at[3 * layer + which])
        for layer in range(2)
        for which, (source, target) in enumerate(((src_hbm, src), (pr_hbm, pr), (pi_hbm, pi)))
    ]
    for load in loads:
        load.start()

    def columns_of(b):
        return pl.ds(pl.multiple_of(b * width, width), width)

    def modes_of(piece):
        return pl.ds(piece * depth, depth)

    def forward_copy(b, piece):
        part = (slice(None), columns_of(b), modes_of(piece))
        return pltpu.make_async_remote_copy(
            src_ref=fout.at[part], dst_ref=fin.at[part],
            send_sem=fsend.at[b * PIECES + piece], recv_sem=frecv.at[b * PIECES + piece],
            device_id={"strip": after}, device_id_type=MESH,
        )

    def backward_copy(b, piece):
        part = (slice(None), columns_of(b), modes_of(piece))
        return pltpu.make_async_remote_copy(
            src_ref=bout.at[part], dst_ref=bin_.at[part],
            send_sem=bsend.at[b * PIECES + piece], recv_sem=brecv.at[b * PIECES + piece],
            device_id={"strip": before}, device_id_type=MESH,
        )

    def pass_on(b, copy, arriving, known, real_part, imag_part, emit):
        part = columns_of(b)
        total = known[:, part, :]
        for piece in range(PIECES - 1):
            copy(b, piece).wait_recv()
            total = total + complex_rows(
                arriving[:, part, modes_of(piece)],
                real_part[modes_of(piece), :], imag_part[modes_of(piece), :], PLAIN,
            )
        copy(b, PIECES - 1).wait_recv()
        ending = modes_of(PIECES - 1)
        vectors = arriving[:, part, ending]
        for piece in range(PIECES):
            lanes = modes_of(piece)
            emit(
                piece, (slice(None), part, lanes),
                total[:, :, piece * depth : (piece + 1) * depth]
                + complex_rows(vectors, real_part[ending, lanes], imag_part[ending, lanes], PLAIN),
            )

    for load in loads[:3]:
        load.wait()
    trace = complex_rows(src[0], pr[0], pi[0], ACROSS)
    for load in loads[3:]:
        load.wait()
    summed = (src[1].astype(F32) + trace).astype(BF16)
    last_trace[...] = complex_rows(summed, pr[1], pi[1], ACROSS)

    inner = jnp.logical_not(jnp.logical_or(is_first, is_last))

    @pl.when(inner)
    def _():
        pl.semaphore_wait(barrier, 2)

    @pl.when(jnp.logical_not(inner))
    def _():
        pl.semaphore_wait(barrier, 1)

    def each(body):
        def step(b, carry):
            body(b)
            return carry

        lax.fori_loop(0, batches, step, 0)

    @pl.when(is_first)
    def _():
        @each
        def _(b):
            part = columns_of(b)
            fout[:, part, :] = last_trace[:, part, :].astype(BF16)
            for piece in range(PIECES):
                forward_copy(b, piece).start()

    def product_rows(left_r, left_i, right_r, right_i):
        real = jnp.dot(left_r, right_r, preferred_element_type=F32) - jnp.dot(
            left_i, right_i, preferred_element_type=F32
        )
        imag = jnp.dot(left_r, right_i, preferred_element_type=F32) + jnp.dot(
            left_i, right_r, preferred_element_type=F32
        )
        return real, imag

    def build(target_r, target_i, compute):
        def step(i, carry):
            block = pl.ds(pl.multiple_of(i * BLOCK, BLOCK), BLOCK)
            real, imag = compute(block)
            target_r[:, block] = real.T.astype(BF16)
            target_i[:, block] = imag.T.astype(BF16)
            return carry

        lax.fori_loop(0, modes // BLOCK, step, 0)

    def forward_rows(block):
        return product_rows(pr[1, block, :], pi[1, block, :], pr[0], pi[0])

    def backward_rows(block):
        return product_rows(pr[0, block, :], pi[0, block, :], pr[1], pi[1])

    def turn_rows(block):
        real, imag = backward_rows(block)
        real, imag = product_rows(real.astype(BF16), imag.astype(BF16), pr[0], pi[0])
        return real + pr[0, block, :].astype(F32), imag + pi[0, block, :].astype(F32)

    early = me < strips // 2

    second = jnp.logical_and(inner, me == 1)
    later = jnp.logical_and(inner, me != 1)

    @pl.when(second)
    def _():
        def direct(g, carry):
            for b in range(GROUP):
                for piece in range(PIECES):
                    forward_copy(g * GROUP + b, piece).wait_recv()
            part = pl.ds(pl.multiple_of(g * (GROUP * width), width), GROUP * width)
            summed = (src[0, :, part, :].astype(F32) + fin[:, part, :].astype(F32)).astype(BF16)
            trace = complex_rows(summed, pr[0], pi[0], ACROSS)
            summed = (src[1, :, part, :].astype(F32) + trace).astype(BF16)
            trace = complex_rows(summed, pr[1], pi[1], ACROSS)
            fout[:, part, :] = trace.astype(BF16)
            for b in range(GROUP):
                for piece in range(PIECES):
                    forward_copy(g * GROUP + b, piece).start()
            last_trace[:, part, :] = trace
            return carry

        lax.fori_loop(0, batches // GROUP, direct, 0)

    @pl.when(later)
    def _():
        build(fwd_r, fwd_i, forward_rows)

    @pl.when(jnp.logical_and(inner, jnp.logical_not(early)))
    def _():
        build(bwd_r, bwd_i, backward_rows)

    @pl.when(later)
    def _():
        @each
        def _(b):
            def emit(piece, part, total):
                fout[part] = total.astype(BF16)
                forward_copy(b, piece).start()
                last_trace[part] = total

            pass_on(b, forward_copy, fin, last_trace, fwd_r, fwd_i, emit)

    @pl.when(is_last)
    def _():
        build(bwd_r, bwd_i, turn_rows)
        known = src[0].astype(F32) + last_trace[...]
        base[...] = complex_rows(known.astype(BF16), pr[0], pi[0], ACROSS)

        @each
        def _(b):
            def emit(piece, part, total):
                field = total.astype(BF16)
                bout[part] = field
                backward_copy(b, piece).start()
                out[(0,) + part] = field

            pass_on(b, forward_copy, fin, base, bwd_r, bwd_i, emit)

        passed = complex_rows(fin[...], pr[0], pi[0], ACROSS).astype(BF16)
        field = last_trace[...] + complex_rows(passed, pr[1], pi[1], ACROSS)
        out[1] = field.astype(BF16)

    @pl.when(inner)
    def _():
        known = src[0].astype(F32) + fin[...].astype(F32) + last_trace[...]
        base[...] = complex_rows(known.astype(BF16), pr[0], pi[0], ACROSS)

    @pl.when(is_first)
    def _():
        known = src[0].astype(F32) + last_trace[...]
        base[...] = complex_rows(known.astype(BF16), pr[0], pi[0], ACROSS)

    @pl.when(jnp.logical_and(early, jnp.logical_not(is_last)))
    def _():
        build(bwd_r, bwd_i, backward_rows)

    @pl.when(jnp.logical_not(is_last))
    def _():
        @each
        def _(b):
            def emit(piece, part, total):
                field = total.astype(BF16)

                @pl.when(jnp.logical_not(is_first))
                def _():
                    bout[part] = field
                    backward_copy(b, piece).start()

                out[(0,) + part] = field

            pass_on(b, backward_copy, bin_, base, bwd_r, bwd_i, emit)

        field = last_trace[...] + complex_rows(bin_[...], pr[1], pi[1], ACROSS)
        out[1] = field.astype(BF16)

        @each
        def _(b):
            for piece in range(PIECES):
                forward_copy(b, piece).wait_send()

    @pl.when(jnp.logical_not(is_first))
    def _():
        @each
        def _(b):
            for piece in range(PIECES):
                backward_copy(b, piece).wait_send()


def solution(mesh):
    strips = mesh.shape["strip"]

    def step(source, pivot_inverse_real, factor_imag):
        layers, modes, halves, columns = source.shape
        placed = source.transpose(0, 2, 3, 1)
        anywhere = pl.BlockSpec(memory_space=pl.ANY)
        vectors = (halves, columns, modes)
        chunked = (layers,) + vectors
        square = (modes, modes)
        result = pl.pallas_call(
            functools.partial(kernel, strips),
            out_shape=jax.ShapeDtypeStruct(chunked, BF16),
            in_specs=[anywhere] * 3,
            out_specs=pl.BlockSpec(memory_space=pltpu.VMEM),
            scratch_shapes=[
                pltpu.VMEM(chunked, BF16),
                pltpu.VMEM((layers,) + square, BF16),
                pltpu.VMEM((layers,) + square, BF16),
            ]
            + [pltpu.VMEM(square, BF16)] * 4
            + [pltpu.VMEM(vectors, F32)] * 2
            + [pltpu.VMEM(vectors, BF16)] * 4
            + [pltpu.SemaphoreType.DMA((6,))]
            + [pltpu.SemaphoreType.DMA((BATCHES * PIECES,))] * 4,
            compiler_params=pltpu.CompilerParams(
                collective_id=0, has_side_effects=True, vmem_limit_bytes=56 * 1024 * 1024
            ),
        )(placed, pivot_inverse_real, factor_imag)
        return result.transpose(0, 3, 1, 2)

    return jax.shard_map(
        step,
        mesh=mesh,
        in_specs=(P("strip", None, None, "wave"), P("strip", "wave", None), P("strip", "wave", None)),
        out_specs=P("strip", None, None, "wave"),
        check_vma=False,
    )
```

```python
import functools

import jax
import jax.numpy as jnp
from jax import lax
from jax.experimental import pallas as pl
from jax.experimental.pallas import tpu as pltpu
from jax.sharding import PartitionSpec as P

BATCHES = 8
PIECES = 2
GROUP = 2
BLOCK = 256
F32 = jnp.float32
BF16 = jnp.bfloat16
MESH = pl.DeviceIdType.MESH
PLAIN = (((1,), (0,)), ((), ()))
ACROSS = (((1,), (1,)), ((), ()))


def combine(direct, crossed):
    return jnp.stack([direct[0] - crossed[1], direct[1] + crossed[0]])


def complex_rows(vectors, real_part, imag_part, dims):
    halves, columns, modes = vectors.shape
    merged = vectors.reshape(halves * columns, modes)
    outcome = (halves, columns, real_part.shape[1 - dims[0][1][0]])
    direct = lax.dot_general(merged, real_part, dims, preferred_element_type=F32).reshape(outcome)
    crossed = lax.dot_general(merged, imag_part, dims, preferred_element_type=F32).reshape(outcome)
    return combine(direct, crossed)


def kernel(
    strips, src_hbm, pr_hbm, pi_hbm, out, src, pr, pi, fwd_r, fwd_i, bwd_r, bwd_i, last_trace, base,
    fin, fout, bin_, bout, load_sem, fsend, frecv, bsend, brecv,
):
    me = lax.axis_index("strip")
    halves, columns, modes = fin.shape
    batches = BATCHES
    width = columns // batches
    depth = modes // PIECES
    is_first, is_last = me == 0, me == strips - 1
    after, before = jnp.minimum(me + 1, strips - 1), jnp.maximum(me - 1, 0)
    barrier = pltpu.get_barrier_semaphore()

    @pl.when(jnp.logical_not(is_first))
    def _():
        pl.semaphore_signal(barrier, inc=1, device_id={"strip": before}, device_id_type=MESH)

    @pl.when(jnp.logical_not(is_last))
    def _():
        pl.semaphore_signal(barrier, inc=1, device_id={"strip": after}, device_id_type=MESH)

    loads = [
        pltpu.make_async_copy(source.at[layer], target.at[layer], load_sem.at[3 * layer + which])
        for layer in range(2)
        for which, (source, target) in enumerate(((src_hbm, src), (pr_hbm, pr), (pi_hbm, pi)))
    ]
    for load in loads:
        load.start()

    def columns_of(b):
        return pl.ds(pl.multiple_of(b * width, width), width)

    def modes_of(piece):
        return pl.ds(piece * depth, depth)

    def forward_copy(b, piece):
        part = (slice(None), columns_of(b), modes_of(piece))
        return pltpu.make_async_remote_copy(
            src_ref=fout.at[part], dst_ref=fin.at[part],
            send_sem=fsend.at[b * PIECES + piece], recv_sem=frecv.at[b * PIECES + piece],
            device_id={"strip": after}, device_id_type=MESH,
        )

    def backward_copy(b, piece):
        part = (slice(None), columns_of(b), modes_of(piece))
        return pltpu.make_async_remote_copy(
            src_ref=bout.at[part], dst_ref=bin_.at[part],
            send_sem=bsend.at[b * PIECES + piece], recv_sem=brecv.at[b * PIECES + piece],
            device_id={"strip": before}, device_id_type=MESH,
        )

    def pass_on(b, copy, arriving, known, real_part, imag_part, emit):
        part = columns_of(b)
        total = known[:, part, :]
        for piece in range(PIECES - 1):
            copy(b, piece).wait_recv()
            total = total + complex_rows(
                arriving[:, part, modes_of(piece)],
                real_part[modes_of(piece), :], imag_part[modes_of(piece), :], PLAIN,
            )
        copy(b, PIECES - 1).wait_recv()
        ending = modes_of(PIECES - 1)
        vectors = arriving[:, part, ending]
        for piece in range(PIECES):
            lanes = modes_of(piece)
            emit(
                piece, (slice(None), part, lanes),
                total[:, :, piece * depth : (piece + 1) * depth]
                + complex_rows(vectors, real_part[ending, lanes], imag_part[ending, lanes], PLAIN),
            )

    for load in loads[:3]:
        load.wait()
    trace = complex_rows(src[0], pr[0], pi[0], ACROSS)
    for load in loads[3:]:
        load.wait()
    summed = (src[1].astype(F32) + trace).astype(BF16)
    last_trace[...] = complex_rows(summed, pr[1], pi[1], ACROSS)

    inner = jnp.logical_not(jnp.logical_or(is_first, is_last))

    @pl.when(inner)
    def _():
        pl.semaphore_wait(barrier, 2)

    @pl.when(jnp.logical_not(inner))
    def _():
        pl.semaphore_wait(barrier, 1)

    def each(body):
        def step(b, carry):
            body(b)
            return carry

        lax.fori_loop(0, batches, step, 0)

    @pl.when(is_first)
    def _():
        @each
        def _(b):
            part = columns_of(b)
            fout[:, part, :] = last_trace[:, part, :].astype(BF16)
            for piece in range(PIECES):
                forward_copy(b, piece).start()

    def product_rows(left_r, left_i, right_r, right_i):
        real = jnp.dot(left_r, right_r, preferred_element_type=F32) - jnp.dot(
            left_i, right_i, preferred_element_type=F32
        )
        imag = jnp.dot(left_r, right_i, preferred_element_type=F32) + jnp.dot(
            left_i, right_r, preferred_element_type=F32
        )
        return real, imag

    def build(target_r, target_i, compute):
        def step(i, carry):
            block = pl.ds(pl.multiple_of(i * BLOCK, BLOCK), BLOCK)
            real, imag = compute(block)
            target_r[:, block] = real.T.astype(BF16)
            target_i[:, block] = imag.T.astype(BF16)
            return carry

        lax.fori_loop(0, modes // BLOCK, step, 0)

    def forward_rows(block):
        return product_rows(pr[1, block, :], pi[1, block, :], pr[0], pi[0])

    def backward_rows(block):
        return product_rows(pr[0, block, :], pi[0, block, :], pr[1], pi[1])

    def turn_rows(block):
        real, imag = backward_rows(block)
        real, imag = product_rows(real.astype(BF16), imag.astype(BF16), pr[0], pi[0])
        return real + pr[0, block, :].astype(F32), imag + pi[0, block, :].astype(F32)

    early = me < strips - 3

    second = jnp.logical_and(inner, me == 1)
    later = jnp.logical_and(inner, me != 1)

    @pl.when(second)
    def _():
        def direct(g, carry):
            for b in range(GROUP):
                for piece in range(PIECES):
                    forward_copy(g * GROUP + b, piece).wait_recv()
            part = pl.ds(pl.multiple_of(g * (GROUP * width), width), GROUP * width)
            summed = (src[0, :, part, :].astype(F32) + fin[:, part, :].astype(F32)).astype(BF16)
            trace = complex_rows(summed, pr[0], pi[0], ACROSS)
            summed = (src[1, :, part, :].astype(F32) + trace).astype(BF16)
            trace = complex_rows(summed, pr[1], pi[1], ACROSS)
            fout[:, part, :] = trace.astype(BF16)
            for b in range(GROUP):
                for piece in range(PIECES):
                    forward_copy(g * GROUP + b, piece).start()
            last_trace[:, part, :] = trace
            return carry

        lax.fori_loop(0, batches // GROUP, direct, 0)

    @pl.when(later)
    def _():
        build(fwd_r, fwd_i, forward_rows)

    @pl.when(jnp.logical_and(inner, jnp.logical_not(early)))
    def _():
        build(bwd_r, bwd_i, backward_rows)

    @pl.when(later)
    def _():
        @each
        def _(b):
            def emit(piece, part, total):
                fout[part] = total.astype(BF16)
                forward_copy(b, piece).start()
                last_trace[part] = total

            pass_on(b, forward_copy, fin, last_trace, fwd_r, fwd_i, emit)

    @pl.when(is_last)
    def _():
        build(bwd_r, bwd_i, turn_rows)
        known = src[0].astype(F32) + last_trace[...]
        base[...] = complex_rows(known.astype(BF16), pr[0], pi[0], ACROSS)

        @each
        def _(b):
            def emit(piece, part, total):
                field = total.astype(BF16)
                bout[part] = field
                backward_copy(b, piece).start()
                out[(0,) + part] = field

            pass_on(b, forward_copy, fin, base, bwd_r, bwd_i, emit)

        passed = complex_rows(fin[...], pr[0], pi[0], ACROSS).astype(BF16)
        field = last_trace[...] + complex_rows(passed, pr[1], pi[1], ACROSS)
        out[1] = field.astype(BF16)

    @pl.when(inner)
    def _():
        known = src[0].astype(F32) + fin[...].astype(F32) + last_trace[...]
        base[...] = complex_rows(known.astype(BF16), pr[0], pi[0], ACROSS)

    @pl.when(is_first)
    def _():
        known = src[0].astype(F32) + last_trace[...]
        base[...] = complex_rows(known.astype(BF16), pr[0], pi[0], ACROSS)

    @pl.when(jnp.logical_and(early, jnp.logical_not(is_last)))
    def _():
        build(bwd_r, bwd_i, backward_rows)

    @pl.when(jnp.logical_not(is_last))
    def _():
        @each
        def _(b):
            def emit(piece, part, total):
                field = total.astype(BF16)

                @pl.when(jnp.logical_not(is_first))
                def _():
                    bout[part] = field
                    backward_copy(b, piece).start()

                out[(0,) + part] = field

            pass_on(b, backward_copy, bin_, base, bwd_r, bwd_i, emit)

        field = last_trace[...] + complex_rows(bin_[...], pr[1], pi[1], ACROSS)
        out[1] = field.astype(BF16)

        @each
        def _(b):
            for piece in range(PIECES):
                forward_copy(b, piece).wait_send()

    @pl.when(jnp.logical_not(is_first))
    def _():
        @each
        def _(b):
            for piece in range(PIECES):
                backward_copy(b, piece).wait_send()


def solution(mesh):
    strips = mesh.shape["strip"]

    def step(source, pivot_inverse_real, factor_imag):
        layers, modes, halves, columns = source.shape
        placed = source.transpose(0, 2, 3, 1)
        anywhere = pl.BlockSpec(memory_space=pl.ANY)
        vectors = (halves, columns, modes)
        chunked = (layers,) + vectors
        square = (modes, modes)
        result = pl.pallas_call(
            functools.partial(kernel, strips),
            out_shape=jax.ShapeDtypeStruct(chunked, BF16),
            in_specs=[anywhere] * 3,
            out_specs=pl.BlockSpec(memory_space=pltpu.VMEM),
            scratch_shapes=[
                pltpu.VMEM(chunked, BF16),
                pltpu.VMEM((layers,) + square, BF16),
                pltpu.VMEM((layers,) + square, BF16),
            ]
            + [pltpu.VMEM(square, BF16)] * 4
            + [pltpu.VMEM(vectors, F32)] * 2
            + [pltpu.VMEM(vectors, BF16)] * 4
            + [pltpu.SemaphoreType.DMA((6,))]
            + [pltpu.SemaphoreType.DMA((BATCHES * PIECES,))] * 4,
            compiler_params=pltpu.CompilerParams(
                collective_id=0, has_side_effects=True, vmem_limit_bytes=56 * 1024 * 1024
            ),
        )(placed, pivot_inverse_real, factor_imag)
        return result.transpose(0, 3, 1, 2)

    return jax.shard_map(
        step,
        mesh=mesh,
        in_specs=(P("strip", None, None, "wave"), P("strip", "wave", None), P("strip", "wave", None)),
        out_specs=P("strip", None, None, "wave"),
        check_vma=False,
    )
```

```python
import functools

import jax
import jax.numpy as jnp
from jax import lax
from jax.experimental import pallas as pl
from jax.experimental.pallas import tpu as pltpu
from jax.sharding import PartitionSpec as P

BATCHES = 8
PIECES = 2
GROUP = 2
BLOCK = 256
F32 = jnp.float32
BF16 = jnp.bfloat16
MESH = pl.DeviceIdType.MESH
PLAIN = (((1,), (0,)), ((), ()))
ACROSS = (((1,), (1,)), ((), ()))


def combine(direct, crossed):
    return jnp.stack([direct[0] - crossed[1], direct[1] + crossed[0]])


def complex_rows(vectors, real_part, imag_part, dims):
    halves, columns, modes = vectors.shape
    merged = vectors.reshape(halves * columns, modes)
    outcome = (halves, columns, real_part.shape[1 - dims[0][1][0]])
    direct = lax.dot_general(merged, real_part, dims, preferred_element_type=F32).reshape(outcome)
    crossed = lax.dot_general(merged, imag_part, dims, preferred_element_type=F32).reshape(outcome)
    return combine(direct, crossed)


def kernel(
    strips, src_hbm, pr_hbm, pi_hbm, out, src, pr, pi, fwd_r, fwd_i, bwd_r, bwd_i, last_trace, base,
    fin, fout, bin_, bout, load_sem, fsend, frecv, bsend, brecv,
):
    me = lax.axis_index("strip")
    halves, columns, modes = fin.shape
    batches = BATCHES
    width = columns // batches
    depth = modes // PIECES
    is_first, is_last = me == 0, me == strips - 1
    after, before = jnp.minimum(me + 1, strips - 1), jnp.maximum(me - 1, 0)
    barrier = pltpu.get_barrier_semaphore()

    @pl.when(jnp.logical_not(is_first))
    def _():
        pl.semaphore_signal(barrier, inc=1, device_id={"strip": before}, device_id_type=MESH)

    @pl.when(jnp.logical_not(is_last))
    def _():
        pl.semaphore_signal(barrier, inc=1, device_id={"strip": after}, device_id_type=MESH)

    loads = [
        pltpu.make_async_copy(source.at[layer], target.at[layer], load_sem.at[3 * layer + which])
        for layer in range(2)
        for which, (source, target) in enumerate(((src_hbm, src), (pr_hbm, pr), (pi_hbm, pi)))
    ]
    for load in loads:
        load.start()

    def columns_of(b):
        return pl.ds(pl.multiple_of(b * width, width), width)

    def modes_of(piece):
        return pl.ds(piece * depth, depth)

    def forward_copy(b, piece):
        part = (slice(None), columns_of(b), modes_of(piece))
        return pltpu.make_async_remote_copy(
            src_ref=fout.at[part], dst_ref=fin.at[part],
            send_sem=fsend.at[b * PIECES + piece], recv_sem=frecv.at[b * PIECES + piece],
            device_id={"strip": after}, device_id_type=MESH,
        )

    def backward_copy(b, piece):
        part = (slice(None), columns_of(b), modes_of(piece))
        return pltpu.make_async_remote_copy(
            src_ref=bout.at[part], dst_ref=bin_.at[part],
            send_sem=bsend.at[b * PIECES + piece], recv_sem=brecv.at[b * PIECES + piece],
            device_id={"strip": before}, device_id_type=MESH,
        )

    def pass_on(b, copy, arriving, known, real_part, imag_part, emit):
        part = columns_of(b)
        total = known[:, part, :]
        for piece in range(PIECES - 1):
            copy(b, piece).wait_recv()
            total = total + complex_rows(
                arriving[:, part, modes_of(piece)],
                real_part[modes_of(piece), :], imag_part[modes_of(piece), :], PLAIN,
            )
        copy(b, PIECES - 1).wait_recv()
        ending = modes_of(PIECES - 1)
        vectors = arriving[:, part, ending]
        for piece in range(PIECES):
            lanes = modes_of(piece)
            emit(
                piece, (slice(None), part, lanes),
                total[:, :, piece * depth : (piece + 1) * depth]
                + complex_rows(vectors, real_part[ending, lanes], imag_part[ending, lanes], PLAIN),
            )

    for load in loads[:3]:
        load.wait()
    trace = complex_rows(src[0], pr[0], pi[0], ACROSS)
    for load in loads[3:]:
        load.wait()
    summed = (src[1].astype(F32) + trace).astype(BF16)
    last_trace[...] = complex_rows(summed, pr[1], pi[1], ACROSS)

    inner = jnp.logical_not(jnp.logical_or(is_first, is_last))

    @pl.when(inner)
    def _():
        pl.semaphore_wait(barrier, 2)

    @pl.when(jnp.logical_not(inner))
    def _():
        pl.semaphore_wait(barrier, 1)

    def each(body):
        def step(b, carry):
            body(b)
            return carry

        lax.fori_loop(0, batches, step, 0)

    @pl.when(is_first)
    def _():
        @each
        def _(b):
            part = columns_of(b)
            fout[:, part, :] = last_trace[:, part, :].astype(BF16)
            for piece in range(PIECES):
                forward_copy(b, piece).start()

    def product_rows(left_r, left_i, right_r, right_i):
        real = jnp.dot(left_r, right_r, preferred_element_type=F32) - jnp.dot(
            left_i, right_i, preferred_element_type=F32
        )
        imag = jnp.dot(left_r, right_i, preferred_element_type=F32) + jnp.dot(
            left_i, right_r, preferred_element_type=F32
        )
        return real, imag

    def build(target_r, target_i, compute):
        def step(i, carry):
            block = pl.ds(pl.multiple_of(i * BLOCK, BLOCK), BLOCK)
            real, imag = compute(block)
            target_r[:, block] = real.T.astype(BF16)
            target_i[:, block] = imag.T.astype(BF16)
            return carry

        lax.fori_loop(0, modes // BLOCK, step, 0)

    def forward_rows(block):
        return product_rows(pr[1, block, :], pi[1, block, :], pr[0], pi[0])

    def backward_rows(block):
        return product_rows(pr[0, block, :], pi[0, block, :], pr[1], pi[1])

    def turn_rows(block):
        real, imag = backward_rows(block)
        real, imag = product_rows(real.astype(BF16), imag.astype(BF16), pr[0], pi[0])
        return real + pr[0, block, :].astype(F32), imag + pi[0, block, :].astype(F32)

    early = me < strips - 3

    second = jnp.logical_and(inner, me <= 2)
    later = jnp.logical_and(inner, me > 2)

    @pl.when(second)
    def _():
        def direct(g, carry):
            for b in range(GROUP):
                for piece in range(PIECES):
                    forward_copy(g * GROUP + b, piece).wait_recv()
            part = pl.ds(pl.multiple_of(g * (GROUP * width), width), GROUP * width)
            summed = (src[0, :, part, :].astype(F32) + fin[:, part, :].astype(F32)).astype(BF16)
            trace = complex_rows(summed, pr[0], pi[0], ACROSS)
            summed = (src[1, :, part, :].astype(F32) + trace).astype(BF16)
            trace = complex_rows(summed, pr[1], pi[1], ACROSS)
            fout[:, part, :] = trace.astype(BF16)
            for b in range(GROUP):
                for piece in range(PIECES):
                    forward_copy(g * GROUP + b, piece).start()
            last_trace[:, part, :] = trace
            return carry

        lax.fori_loop(0, batches // GROUP, direct, 0)

    @pl.when(later)
    def _():
        build(fwd_r, fwd_i, forward_rows)

    @pl.when(jnp.logical_and(inner, jnp.logical_not(early)))
    def _():
        build(bwd_r, bwd_i, backward_rows)

    @pl.when(later)
    def _():
        @each
        def _(b):
            def emit(piece, part, total):
                fout[part] = total.astype(BF16)
                forward_copy(b, piece).start()
                last_trace[part] = total

            pass_on(b, forward_copy, fin, last_trace, fwd_r, fwd_i, emit)

    @pl.when(is_last)
    def _():
        build(bwd_r, bwd_i, turn_rows)
        known = src[0].astype(F32) + last_trace[...]
        base[...] = complex_rows(known.astype(BF16), pr[0], pi[0], ACROSS)

        @each
        def _(b):
            def emit(piece, part, total):
                field = total.astype(BF16)
                bout[part] = field
                backward_copy(b, piece).start()
                out[(0,) + part] = field

            pass_on(b, forward_copy, fin, base, bwd_r, bwd_i, emit)

        passed = complex_rows(fin[...], pr[0], pi[0], ACROSS).astype(BF16)
        field = last_trace[...] + complex_rows(passed, pr[1], pi[1], ACROSS)
        out[1] = field.astype(BF16)

    @pl.when(inner)
    def _():
        known = src[0].astype(F32) + fin[...].astype(F32) + last_trace[...]
        base[...] = complex_rows(known.astype(BF16), pr[0], pi[0], ACROSS)

    @pl.when(is_first)
    def _():
        known = src[0].astype(F32) + last_trace[...]
        base[...] = complex_rows(known.astype(BF16), pr[0], pi[0], ACROSS)

    @pl.when(jnp.logical_and(early, jnp.logical_not(is_last)))
    def _():
        build(bwd_r, bwd_i, backward_rows)

    @pl.when(jnp.logical_not(is_last))
    def _():
        @each
        def _(b):
            def emit(piece, part, total):
                field = total.astype(BF16)

                @pl.when(jnp.logical_not(is_first))
                def _():
                    bout[part] = field
                    backward_copy(b, piece).start()

                out[(0,) + part] = field

            pass_on(b, backward_copy, bin_, base, bwd_r, bwd_i, emit)

        field = last_trace[...] + complex_rows(bin_[...], pr[1], pi[1], ACROSS)
        out[1] = field.astype(BF16)

        @each
        def _(b):
            for piece in range(PIECES):
                forward_copy(b, piece).wait_send()

    @pl.when(jnp.logical_not(is_first))
    def _():
        @each
        def _(b):
            for piece in range(PIECES):
                backward_copy(b, piece).wait_send()


def solution(mesh):
    strips = mesh.shape["strip"]

    def step(source, pivot_inverse_real, factor_imag):
        layers, modes, halves, columns = source.shape
        placed = source.transpose(0, 2, 3, 1)
        anywhere = pl.BlockSpec(memory_space=pl.ANY)
        vectors = (halves, columns, modes)
        chunked = (layers,) + vectors
        square = (modes, modes)
        result = pl.pallas_call(
            functools.partial(kernel, strips),
            out_shape=jax.ShapeDtypeStruct(chunked, BF16),
            in_specs=[anywhere] * 3,
            out_specs=pl.BlockSpec(memory_space=pltpu.VMEM),
            scratch_shapes=[
                pltpu.VMEM(chunked, BF16),
                pltpu.VMEM((layers,) + square, BF16),
                pltpu.VMEM((layers,) + square, BF16),
            ]
            + [pltpu.VMEM(square, BF16)] * 4
            + [pltpu.VMEM(vectors, F32)] * 2
            + [pltpu.VMEM(vectors, BF16)] * 4
            + [pltpu.SemaphoreType.DMA((6,))]
            + [pltpu.SemaphoreType.DMA((BATCHES * PIECES,))] * 4,
            compiler_params=pltpu.CompilerParams(
                collective_id=0, has_side_effects=True, vmem_limit_bytes=56 * 1024 * 1024
            ),
        )(placed, pivot_inverse_real, factor_imag)
        return result.transpose(0, 3, 1, 2)

    return jax.shard_map(
        step,
        mesh=mesh,
        in_specs=(P("strip", None, None, "wave"), P("strip", "wave", None), P("strip", "wave", None)),
        out_specs=P("strip", None, None, "wave"),
        check_vma=False,
    )
```
